256 devices in a mesh: expert: 32 (over y, x, core), fsdp: 8 (over z).
Axes of the slice: x: 4, y: 4, z: 8, core: 2. Of those that a mesh axis runs over, the one named last changes fastest.
Arguments:
- tokens: bfloat16 [32768, 4096], P(('expert', 'fsdp')), may hold values from -24 to 24
- output_grad: bfloat16 [32768, 4096], P(('expert', 'fsdp')), may hold values from -24 to 24
- combine: bfloat16 [32768, 2], P(('expert', 'fsdp')), may hold values from 0.19921875 to 1
- expert_ids: int32 [32768, 2], P(('expert', 'fsdp')), may hold values from 0 to 7, as said below
- gate_weight: bfloat16 [4096, 14336], P('fsdp', 'expert'), may hold values from -0.09375 to 0.09375
- up_weight: bfloat16 [4096, 14336], P('fsdp', 'expert'), may hold values from -0.09375 to 0.09375
- down_weight: bfloat16 [4096, 14336], P('fsdp', 'expert'), may hold values from -0.0625 to 0.0625
Outputs:
- layer_out: bfloat16 [32768, 4096], P(('expert', 'fsdp'))
- tokens_grad: bfloat16 [32768, 4096], P(('expert', 'fsdp'))
- combine_grad: float32 [32768, 2], P(('expert', 'fsdp'))
- gate_grad: bfloat16 [4096, 14336], P('fsdp', 'expert')
- up_grad: bfloat16 [4096, 14336], P('fsdp', 'expert')
- down_grad: bfloat16 [4096, 14336], P('fsdp', 'expert')
The draws below stay inside these ranges and needn't reach their ends.
Inputs may be any that keep to these rules, and one draw needn't show every extreme that they name: `expert_ids`: each row names 2 different experts. Among the 128 rows of one device, each expert below 2 is named by 1 to 4 rows; in every draw there is an fsdp index for which the rows of every device with that index name one of those experts exactly 4 times.
All inputs are finite; a program needn't handle non-finite values.
Results may differ from the reference program's by a relative error of at most 0.013.
Values may be sent and summed in bfloat16 or wider, within the bound.
No kernel may reach another device: no remote copies, remote signals or barrier semaphores. Data moves between devices by JAX's collectives and lax.ppermute only.
A program may use at most 128 MiB of HBM per device.

```python
import jax
import jax.numpy as jnp
from jax import lax

D = 4096
FF = 7168
EXPERTS_ALL = 8
WIN = 2
TOPK = 2
TOK_DEV = 128
SLOTS = 4
HSPLIT = 16
FF_DEV = 448
HID = 14336
TOKENS = 32768
N_EXPERT = 32
N_FSDP = 8
DEVICES = 256


def draw_expert_ids(key, part):
    keys = jax.random.split(jax.random.fold_in(key, 17), 6)
    counts = jax.random.randint(keys[0], (DEVICES, WIN), 1, SLOTS + 1)
    full_column = jax.random.randint(keys[1], (), 0, N_FSDP)
    full_expert = jax.random.randint(keys[2], (), 0, WIN)
    column_of = jnp.arange(DEVICES, dtype=jnp.int32) % N_FSDP
    forced = (column_of[:, None] == full_column) & (jnp.arange(WIN, dtype=jnp.int32)[None, :] == full_expert)
    counts = jnp.where(forced, SLOTS, counts)
    scores = jax.random.randint(keys[3], (DEVICES, WIN, TOK_DEV), 0, 1 << 16) * TOK_DEV + jnp.arange(TOK_DEV, dtype=jnp.int32)
    ranks = jnp.argsort(jnp.argsort(scores, axis=-1), axis=-1)
    picked = ranks < counts[:, :, None]
    picked_tokens = jnp.transpose(picked, (0, 2, 1)).reshape(DEVICES * TOK_DEV, WIN)
    others = EXPERTS_ALL - WIN
    other_scores = jax.random.randint(keys[4], (DEVICES * TOK_DEV, others), 0, 1 << 16) * others + jnp.arange(others, dtype=jnp.int32)
    named = (jnp.argsort(-other_scores, axis=-1)[:, :TOPK] + WIN).astype(jnp.int32)
    window_ids = jnp.arange(WIN, dtype=jnp.int32)[None, :]
    named = named.at[:, :WIN].set(jnp.where(picked_tokens, window_ids, named[:, :WIN]))
    order_scores = jax.random.randint(keys[5], (DEVICES * TOK_DEV, TOPK), 0, 1 << 16) * TOPK + jnp.arange(TOPK, dtype=jnp.int32)
    column_order = jnp.argsort(order_scores, axis=-1)
    return jnp.take_along_axis(named, column_order, axis=1).astype(jnp.int32)


def with_spikes(values, rng, source, target, shards_of, factor):
    def block_of(axis_at):
        return (jnp.arange(values.shape[axis_at]) // (values.shape[axis_at] // shards_of)).reshape((-1,) + (1,) * (values.ndim - 1 - axis_at))

    one_side = jax.random.permutation(rng, shards_of)[block_of(target)]
    second = (block_of(target) + shards_of // 2) % shards_of
    return jnp.where((block_of(source) == one_side) | (block_of(source) == second), factor * values, values)


def levels(stream_key, dims, shards, low, largest):
    factor_of = 1.0
    for dim, parts in shards:
        draws = jax.random.uniform(jax.random.fold_in(jax.random.fold_in(stream_key, 6), dim), (parts,), jnp.float32, low / len(shards), largest / len(shards))
        factor_of = factor_of * jnp.repeat(jnp.exp(draws), dims[dim] // parts).reshape((-1,) + (1,) * (len(dims) - 1 - dim))
    return factor_of


def gaussian(rng, extent, scale, bound, shards=(), held_as=jnp.bfloat16):
    entries = scale * jax.random.normal(rng, extent, jnp.float32)
    if shards:
        entries = entries * levels(rng, extent, shards, -0.22, 0.18)
    return jnp.clip(entries, -bound, bound).astype(held_as)


def gaussian_with(stream_key, extent, scale, limit, pieces, heavy, kind=jnp.bfloat16):
    values = scale * jax.random.normal(stream_key, extent, jnp.float32)
    if pieces:
        values = values * levels(stream_key, extent, pieces, -0.22, 0.18)
    return jnp.clip(with_spikes(values, jax.random.fold_in(stream_key, 3), *heavy), -limit, limit).astype(kind)


def setup_inputs(seed: int = 0) -> dict:
    key_list = jax.random.split(jax.random.key(seed), 8)
    return {
        "tokens": gaussian_with(key_list[0], (TOKENS, D), 1.0, 24.0, ((0, 256),), (0, 1, 256, 6.0)),
        "output_grad": gaussian_with(key_list[1], (TOKENS, D), 1.0, 24.0, ((0, 256),), (0, 1, 256, 6.0)),
        "combine": jnp.clip(0.19921875 + 0.80078125 * jax.random.uniform(key_list[2], (TOKENS, TOPK), jnp.float32) ** levels(key_list[2], (TOKENS, TOPK), ((0, 256),), -0.2, 0.2), 0.19921875, 1.0).astype(jnp.bfloat16),
        "expert_ids": draw_expert_ids(jax.random.fold_in(key_list[7], 71), 0),
        "gate_weight": gaussian(key_list[4], (D, HID), D ** -0.5, 0.09375, ((0, 8), (1, 32))),
        "up_weight": gaussian(key_list[5], (D, HID), D ** -0.5, 0.09375, ((0, 8), (1, 32))),
        "down_weight": gaussian(key_list[6], (D, HID), FF ** -0.5, 0.0625, ((0, 8), (1, 32))),
    }


def gather_slots(values, indices):
    return jnp.take(values, indices, axis=0)


def select_rows(expert_ids, combine, expert):
    id_blocks = expert_ids.reshape(N_EXPERT * N_FSDP, TOK_DEV, TOPK)
    combine_blocks = combine.astype(jnp.float32).reshape(N_EXPERT * N_FSDP, TOK_DEV, TOPK)
    matches = id_blocks == expert
    chosen = jnp.any(matches, axis=2)
    weight = jnp.sum(jnp.where(matches, combine_blocks, 0.0), axis=2)
    places = (jnp.cumsum(chosen.astype(jnp.int32), axis=1) - 1).astype(jnp.int32)
    slot_index = jnp.arange(SLOTS, dtype=jnp.int32)
    picker = chosen[:, None, :] & (places[:, None, :] == slot_index[None, :, None])
    token_index = jnp.arange(TOK_DEV, dtype=jnp.int32)
    slot_token = jnp.sum(jnp.where(picker, token_index[None, None, :], 0), axis=2).astype(jnp.int32)
    slot_live = jnp.any(picker, axis=2)
    return matches, chosen, weight, places, slot_token, slot_live


def group_parts(pairs):
    row_total = pairs[0][0].shape[0]
    width_out = pairs[0][1].shape[0]

    def one_group(running, group_index):
        first_unit = group_index * FF_DEV
        group_term = jnp.zeros((row_total, width_out), jnp.float32)
        for left_side, right_side in pairs:
            left_part = lax.dynamic_slice_in_dim(left_side, first_unit, FF_DEV, 1)
            right_part = lax.dynamic_slice_in_dim(right_side, first_unit, FF_DEV, 1)
            group_term = group_term + lax.dot_general(left_part, right_part, (((1,), (1,)), ((), ())), preferred_element_type=jnp.float32)
        rounded = lax.optimization_barrier(group_term.astype(jnp.bfloat16))
        return running + rounded.astype(jnp.float32), None

    summed, unused = lax.scan(one_group, jnp.zeros((row_total, width_out), jnp.float32), jnp.arange(HSPLIT, dtype=jnp.int32))
    return summed


def column_grads(rows_left, rows_right):
    left_cols = rows_left.reshape(N_EXPERT, N_FSDP, SLOTS, rows_left.shape[1])
    right_cols = rows_right.reshape(N_EXPERT, N_FSDP, SLOTS, rows_right.shape[1])
    summed = jnp.zeros((rows_left.shape[1], rows_right.shape[1]), jnp.float32)
    for column in range(N_FSDP):
        left_part = left_cols[:, column].reshape(-1, rows_left.shape[1])
        right_part = right_cols[:, column].reshape(-1, rows_right.shape[1])
        column_term = lax.dot_general(left_part, right_part, (((0,), (0,)), ((), ())), preferred_element_type=jnp.float32)
        summed = summed + lax.optimization_barrier(column_term.astype(jnp.bfloat16)).astype(jnp.float32)
    return summed.astype(jnp.bfloat16)


def reference(tokens, output_grad, combine, expert_ids, gate_weight, up_weight, down_weight):
    blocks = N_EXPERT * N_FSDP
    token_blocks = tokens.reshape(blocks, TOK_DEV, D)
    grad_blocks = output_grad.reshape(blocks, TOK_DEV, D)
    grad_float = grad_blocks.astype(jnp.float32)
    many_gather = jax.vmap(gather_slots)
    layer_acc = jnp.zeros((blocks, TOK_DEV, D), jnp.float32)
    input_acc = jnp.zeros((blocks, TOK_DEV, D), jnp.float32)
    combine_acc = jnp.zeros((blocks, TOK_DEV, TOPK), jnp.float32)
    gate_parts, up_parts, down_parts = [], [], []
    for expert in range(WIN):
        matches, chosen, weight, places, slot_token, slot_live = select_rows(expert_ids, combine, expert)
        rows_x = jnp.where(slot_live[:, :, None], many_gather(token_blocks, slot_token), jnp.zeros((), jnp.bfloat16)).reshape(-1, D)
        rows_grad = jnp.where(slot_live[:, :, None], many_gather(grad_blocks, slot_token), jnp.zeros((), jnp.bfloat16)).reshape(-1, D)
        slot_weight = jnp.where(slot_live, many_gather(weight, slot_token), 0.0).reshape(-1, 1)
        gate_cols = gate_weight[:, expert * FF:(expert + 1) * FF]
        up_cols = up_weight[:, expert * FF:(expert + 1) * FF]
        down_cols = down_weight[:, expert * FF:(expert + 1) * FF]
        gate_pre = jnp.dot(rows_x, gate_cols, preferred_element_type=jnp.float32)
        up_pre = jnp.dot(rows_x, up_cols, preferred_element_type=jnp.float32)
        sigma = jax.nn.sigmoid(gate_pre)
        active = gate_pre * sigma
        hidden = (active * up_pre).astype(jnp.bfloat16)
        expert_out = group_parts([(hidden, down_cols)])
        back = slot_weight * jnp.dot(rows_grad, down_cols, preferred_element_type=jnp.float32)
        grad_up = (back * active).astype(jnp.bfloat16)
        grad_gate = (back * up_pre * sigma * (1.0 + gate_pre * (1.0 - sigma))).astype(jnp.bfloat16)
        weighted = (slot_weight * active * up_pre).astype(jnp.bfloat16)
        input_part = group_parts([(grad_gate, gate_cols), (grad_up, up_cols)])
        safe_slot = jnp.clip(places, 0, SLOTS - 1).astype(jnp.int32)
        out_rows = expert_out.reshape(blocks, SLOTS, D)
        in_rows = input_part.reshape(blocks, SLOTS, D)
        token_out = jnp.where(chosen[:, :, None], many_gather(out_rows, safe_slot), 0.0)
        token_in = jnp.where(chosen[:, :, None], many_gather(in_rows, safe_slot), 0.0)
        layer_acc = layer_acc + weight[:, :, None] * token_out
        input_acc = input_acc + token_in
        inner_prod = jnp.sum(grad_float * token_out, axis=2)
        combine_acc = combine_acc + jnp.where(matches, inner_prod[:, :, None], 0.0)
        gate_parts.append(column_grads(rows_x, grad_gate))
        up_parts.append(column_grads(rows_x, grad_up))
        down_parts.append(column_grads(rows_grad, weighted))
    layer_out = layer_acc.reshape(TOKENS, D).astype(jnp.bfloat16)
    tokens_grad = input_acc.reshape(TOKENS, D).astype(jnp.bfloat16)
    combine_grad = combine_acc.reshape(TOKENS, TOPK)
    gate_grad = jnp.concatenate(gate_parts, axis=1)
    up_grad = jnp.concatenate(up_parts, axis=1)
    down_grad = jnp.concatenate(down_parts, axis=1)
    return (layer_out, tokens_grad, combine_grad, gate_grad, up_grad, down_grad)
```

```python
import jax
import jax.numpy as jnp
from jax import lax
from jax.sharding import Mesh
from jax.sharding import PartitionSpec as P

WIN = 2
SLOTS = 4
F32 = jnp.float32
BF16 = jnp.bfloat16


def dot(left, right, contract):
    return lax.dot_general(left, right, (contract, ((), ())), preferred_element_type=F32)


def pick_rows(combine, expert_ids):
    tok = expert_ids.shape[0]
    combine_float = combine.astype(F32)
    slot_index = jnp.arange(SLOTS, dtype=jnp.int32)
    plain, weighted, chosen_matches = [], [], []
    for expert in range(WIN):
        matches = expert_ids == expert
        chosen = jnp.any(matches, axis=1)
        weight = jnp.sum(jnp.where(matches, combine_float, 0.0), axis=1)
        places = jnp.cumsum(chosen.astype(jnp.int32)) - 1
        picker = chosen[None, :] & (places[None, :] == slot_index[:, None])
        plain.append(picker.astype(F32))
        weighted.append(jnp.where(picker, weight[None, :], 0.0))
        chosen_matches.append(matches)
    return jnp.concatenate(plain), jnp.concatenate(weighted), chosen_matches


def make_shards(nz, nchip):
    up = [(i, (i + 1) % nz) for i in range(nz)]
    down = [(i, (i - 1) % nz) for i in range(nz)]
    half = nz // 2

    def to_owners(rows):
        width = rows.shape[1]
        cut = rows.reshape(WIN, SLOTS, nz, width // nz).transpose(0, 2, 1, 3)
        cut = cut.reshape(WIN * nz, SLOTS, width // nz)
        got = lax.all_to_all(cut, ("w", "z"), 0, 0, tiled=True)
        return got.reshape(WIN * nz * SLOTS, width // nz)

    def spread(rows):
        many = jnp.broadcast_to(rows[None], (nchip,) + rows.shape)
        own = lax.all_to_all(many, ("yl", "x"), 0, 0, tiled=True)
        other = lax.ppermute(own, "c", [(0, 1), (1, 0)])
        return jnp.concatenate([own, other], axis=1)

    def collect(parts):
        mid = parts.shape[1] // 2
        other = lax.ppermute(parts[:, mid:].astype(BF16), "c", [(0, 1), (1, 0)])
        own = (parts[:, :mid] + other.astype(F32)).astype(BF16)
        got = lax.all_to_all(own, ("yl", "x"), 0, 0, tiled=True)
        return jnp.sum(got.astype(F32), axis=0).astype(BF16)

    def to_home(rows):
        d = rows.shape[1]
        got = lax.all_to_all(
            rows.reshape(WIN * nz, SLOTS, d), ("w", "z"), 0, 0, tiled=True
        )
        return got.reshape(WIN, nz, SLOTS, d).transpose(0, 2, 1, 3).reshape(WIN * SLOTS, nz * d)

    def ring_reduce(part_of, me):
        going_up = part_of(me + half).astype(BF16)
        going_down = part_of(me - half + 1).astype(BF16)
        for step in range(1, half + 1):
            up_got = lax.ppermute(going_up, "z", up)
            if step < half:
                down_got = lax.ppermute(going_down, "z", down)
                going_up = (part_of(me + half - step) + up_got.astype(F32)).astype(BF16)
                if step < half - 1:
                    going_down = (part_of(me - half + 1 + step) + down_got.astype(F32)).astype(BF16)
        return part_of(me) + up_got.astype(F32) + down_got.astype(F32)

    def ring_gather(mine, me):
        whole = jnp.zeros((nz,) + mine.shape, mine.dtype)
        put = lambda whole, block, at: lax.dynamic_update_slice(
            whole, block[None], (lax.rem(at + 2 * nz, nz), 0, 0)
        )
        whole = put(whole, mine, me)
        from_down, from_up = mine, mine
        for step in range(1, half + 1):
            from_down = lax.ppermute(from_down, "z", up)
            whole = put(whole, from_down, me - step)
            if step < half:
                from_up = lax.ppermute(from_up, "z", down)
                whole = put(whole, from_up, me + step)
        return whole

    def shards(tokens, output_grad, combine, expert_ids, gate_weight, up_weight, down_weight):
        me = lax.axis_index("z")
        hidden_dev = gate_weight.shape[1]
        plain, weighted, matches = pick_rows(combine, expert_ids)
        plain_b, weighted_b = plain.astype(BF16), weighted.astype(BF16)
        rows_x = dot(plain_b, tokens, ((1,), (0,))).astype(BF16)
        rows_g = dot(weighted_b, output_grad, ((1,), (0,))).astype(BF16)
        home_grad = dot(plain_b, output_grad, ((1,), (0,)))

        x_all = spread(to_owners(rows_x))
        g_all = spread(to_owners(rows_g))
        gate_up_weight = jnp.concatenate([gate_weight, up_weight], axis=1)

        def chunk(rows, at):
            at = lax.rem(at + 2 * nz, nz)
            return lax.dynamic_slice_in_dim(rows, at, 1, 0)[0]

        gate_up = ring_reduce(lambda at: dot(chunk(x_all, at), gate_up_weight, ((1,), (0,))), me)
        back = ring_reduce(lambda at: dot(chunk(g_all, at), down_weight, ((1,), (0,))), me)

        gate_pre, up_pre = gate_up[:, :hidden_dev], gate_up[:, hidden_dev:]
        sigma = jax.nn.sigmoid(gate_pre)
        active = gate_pre * sigma
        hidden = (active * up_pre).astype(BF16)
        hidden_all = ring_gather(hidden, me)
        grad_up = (back * active).astype(BF16)
        grad_gate = (back * up_pre * sigma * (1.0 + gate_pre * (1.0 - sigma))).astype(BF16)
        grads_all = ring_gather(jnp.concatenate([grad_gate, grad_up], axis=1), me)

        rows = nchip * x_all.shape[1]
        d = x_all.shape[2]
        flat = lambda a: a.reshape(rows, a.shape[2])
        out_part = dot(flat(hidden_all), down_weight, ((1,), (1,)))
        in_part = dot(flat(grads_all), gate_up_weight, ((1,), (1,)))
        out_rows = to_home(collect(out_part.reshape(nchip, -1, d)))
        in_rows = to_home(collect(in_part.reshape(nchip, -1, d)))

        gate_up_grad = dot(flat(x_all), flat(grads_all), ((0,), (0,))).astype(BF16)
        down_grad = dot(flat(g_all), flat(hidden_all), ((0,), (0,))).astype(BF16)

        layer_out = dot(weighted_b, out_rows, ((0,), (0,))).astype(BF16)
        tokens_grad = dot(plain_b, in_rows, ((0,), (0,))).astype(BF16)
        inner = jnp.sum(home_grad * out_rows.astype(F32), axis=1)
        by_token = plain * inner[:, None]
        combine_grad = jnp.zeros(combine.shape, F32)
        for expert in range(WIN):
            value = jnp.sum(by_token[expert * SLOTS : (expert + 1) * SLOTS], axis=0)
            combine_grad = combine_grad + jnp.where(matches[expert], value[:, None], 0.0)
        return (
            layer_out,
            tokens_grad,
            combine_grad,
            gate_up_grad[:, :hidden_dev],
            gate_up_grad[:, hidden_dev:],
            down_grad,
        )

    return shards


def solution(mesh):
    nexp, nz = mesh.devices.shape
    fine = Mesh(mesh.devices.reshape(WIN, 2, nexp // (4 * WIN), 2, nz), ("w", "yl", "x", "c", "z"))
    expert = ("w", "yl", "x", "c")
    row = P(expert + ("z",), None)
    weight = P("z", expert)
    return jax.shard_map(
        make_shards(nz, nexp // (2 * WIN)),
        mesh=fine,
        in_specs=(row, row, row, row, weight, weight, weight),
        out_specs=(row, row, row, weight, weight, weight),
        check_vma=False,
    )
```

```python
import jax
import jax.numpy as jnp
from jax import lax
from jax.experimental import pallas as pl
from jax.experimental.pallas import tpu as pltpu
from jax.sharding import Mesh
from jax.sharding import PartitionSpec as P

WIN = 2
SLOTS = 4
F32 = jnp.float32
BF16 = jnp.bfloat16
AXES = ("w", "yl", "x", "c", "z")
VMEM = pl.BlockSpec(memory_space=pltpu.VMEM)


def dot(left, right, contract):
    return lax.dot_general(left, right, (contract, ((), ())), preferred_element_type=F32)


def call(body, outs, args, scratch=(), flops=0):
    moved = sum(a.size * a.dtype.itemsize for a in args)
    moved += sum(s.size * s.dtype.itemsize for s in outs)
    return pl.pallas_call(
        body,
        out_shape=outs,
        in_specs=[VMEM] * len(args),
        out_specs=[VMEM] * len(outs),
        scratch_shapes=list(scratch),
        cost_estimate=pl.CostEstimate(flops=flops, bytes_accessed=moved, transcendentals=0),
        compiler_params=pltpu.CompilerParams(vmem_limit_bytes=48 * 1024 * 1024),
    )(*args)


def shaped(shape, dtype=BF16):
    return jax.ShapeDtypeStruct(shape, dtype)


def pick_rows(combine, expert_ids):
    combine_float = combine.astype(F32)
    slot_index = jnp.arange(SLOTS, dtype=jnp.int32)
    plain, weighted, all_matches = [], [], []
    for expert in range(WIN):
        matches = expert_ids == expert
        chosen = jnp.any(matches, axis=1)
        weight = jnp.sum(jnp.where(matches, combine_float, 0.0), axis=1)
        places = jnp.cumsum(chosen.astype(jnp.int32)) - 1
        picker = chosen[None, :] & (places[None, :] == slot_index[:, None])
        plain.append(picker.astype(F32))
        weighted.append(jnp.where(picker, weight[None, :], 0.0))
        all_matches.append(matches)
    return jnp.concatenate(plain), jnp.concatenate(weighted), all_matches


def first_body(own, other, gate_up_w, down_w, own_out, other_out):
    d = gate_up_w.shape[0]
    for rows, out in ((own, own_out), (other, other_out)):
        split = gate_up_w.shape[1]
        out[:, :split] = dot(rows[:, :d], gate_up_w[...], ((1,), (0,))).astype(BF16)
        out[:, split:] = dot(rows[:, d:], down_w[...], ((1,), (0,))).astype(BF16)


def rest_body(own, other, gate_up_w, down_w, out, rows):
    d, split = gate_up_w.shape
    count, half = own.shape[0], own.shape[1]
    for k in range(count):
        rows[k * 2 * half : k * 2 * half + half, :] = own[k]
        rows[k * 2 * half + half : (k + 1) * 2 * half, :] = other[k]
    step = 256
    per = step // (2 * half)
    for s in range(count // per):
        block = rows[s * step : (s + 1) * step, :]
        one = dot(block[:, :d], gate_up_w[...], ((1,), (0,)))
        two = dot(block[:, d:], down_w[...], ((1,), (0,)))
        for p in range(per):
            out[s * per + p, :, :split] = one[p * 2 * half : (p + 1) * 2 * half]
            out[s * per + p, :, split:] = two[p * 2 * half : (p + 1) * 2 * half]


def act_body(part, up_got, down_got, out):
    hid = part.shape[1] // 3

    def total(at):
        cols = slice(at * hid, (at + 1) * hid)
        return part[:, cols] + up_got[:, cols].astype(F32) + down_got[:, cols].astype(F32)

    gate_pre, up_pre, back = total(0), total(1), total(2)
    sigma = jax.nn.sigmoid(gate_pre)
    active = gate_pre * sigma
    out[:, 2 * hid :] = (active * up_pre).astype(BF16)
    out[:, hid : 2 * hid] = (back * active).astype(BF16)
    out[:, :hid] = (back * up_pre * sigma * (1.0 + gate_pre * (1.0 - sigma))).astype(BF16)


def other_body(*refs):
    chunks, (top, bottom, gate_up_w, down_w, own_acts, other_acts, parts) = refs[:7], refs[7:]
    half = top.shape[0]
    places = (0, 1, 2, 3, 5, 6, 7)
    for k, chunk in zip(places, chunks):
        own_acts[k * half : (k + 1) * half, :] = chunk[:half]
        other_acts[k * half : (k + 1) * half, :] = chunk[half:]
    own_acts[4 * half : 5 * half, :] = top[...]
    other_acts[4 * half : 5 * half, :] = bottom[...]
    d, split = gate_up_w.shape
    parts[:, :d] = dot(other_acts[:, :split], gate_up_w[...], ((1,), (1,))).astype(BF16)
    parts[:, d:] = dot(other_acts[:, split:], down_w[...], ((1,), (1,))).astype(BF16)


def own_body(own_acts, gate_up_w, down_w, got, parts):
    d, split = gate_up_w.shape
    one = dot(own_acts[:, :split], gate_up_w[...], ((1,), (1,)))
    parts[:, :d] = (one + got[:, :d].astype(F32)).astype(BF16)
    two = dot(own_acts[:, split:], down_w[...], ((1,), (1,)))
    parts[:, d:] = (two + got[:, d:].astype(F32)).astype(BF16)


def grads_body(own, other, own_acts, other_acts, gate_grad, up_grad, down_grad):
    d, hid = gate_grad.shape
    split = 2 * hid
    both = dot(own[:, :d], own_acts[:, :split], ((0,), (0,)))
    both = both + dot(other[:, :d], other_acts[:, :split], ((0,), (0,)))
    gate_grad[...] = both[:, :hid].astype(BF16)
    up_grad[...] = both[:, hid:].astype(BF16)
    last = dot(own[:, d:], own_acts[:, split:], ((0,), (0,)))
    last = last + dot(other[:, d:], other_acts[:, split:], ((0,), (0,)))
    down_grad[...] = last.astype(BF16)


def make_shards(nz, nchip):
    up = [(i, (i + 1) % nz) for i in range(nz)]
    down = [(i, (i - 1) % nz) for i in range(nz)]
    half = nz // 2
    groups = []
    for w in range(WIN):
        for c in range(2):
            for z in range(nz):
                chips = [(z - k) % nchip for k in range(nchip)]
                groups.append([((w * nchip + chip) * 2 + c) * nz + z for chip in chips])

    def between_chips(blocks):
        return lax.all_to_all(blocks, AXES, 0, 0, axis_index_groups=groups, tiled=True)

    def swap(block):
        return lax.ppermute(block, "c", [(0, 1), (1, 0)])

    def shards(tokens, output_grad, combine, expert_ids, gate_weight, up_weight, down_weight):
        d, hid = gate_weight.shape
        wide = 3 * hid
        plain, weighted, matches = pick_rows(combine, expert_ids)
        plain_b, weighted_b = plain.astype(BF16), weighted.astype(BF16)
        rows_x = dot(plain_b, tokens, ((1,), (0,))).astype(BF16)
        rows_g = dot(weighted_b, output_grad, ((1,), (0,))).astype(BF16)
        cut = lambda rows: rows.reshape(WIN, SLOTS, nz, d).transpose(0, 2, 1, 3)
        send = jnp.concatenate([cut(rows_x), cut(rows_g)], axis=3).reshape(WIN * nz, SLOTS, 2 * d)
        mine = lax.all_to_all(send, ("w", "z"), 0, 0, tiled=True)
        count = WIN * nz * SLOTS
        mine = mine.reshape(count, 2 * d)
        own = between_chips(jnp.broadcast_to(mine[None], (nchip, count, 2 * d)))
        other = swap(own)
        gate_up_w = jnp.concatenate([gate_weight, up_weight], axis=1)
        home_grad = dot(plain_b, output_grad, ((1,), (0,)))

        up_send, down_send = call(
            first_body,
            [shaped((count, wide))] * 2,
            [own[half], other[half], gate_up_w, down_weight],
            flops=4 * count * d * wide,
        )
        up_got = lax.ppermute(up_send, "z", up)
        down_got = lax.ppermute(down_send, "z", down)
        (part,) = call(
            rest_body,
            [shaped((nchip, 2 * count, wide), F32)],
            [own, other, gate_up_w, down_weight],
            scratch=[pltpu.VMEM((nchip * 2 * count, 2 * d), BF16)],
            flops=4 * nchip * count * d * wide,
        )
        for away in range(half - 1, 0, -1):
            up_part, down_part = part[nchip - away], part[away]
            if away == half - 1:
                up_part = jnp.concatenate([up_part[:count] + up_got.astype(F32), up_part[count:]])
                down_part = jnp.concatenate([down_part[:count], down_part[count:] + down_got.astype(F32)])
            else:
                up_part = up_part + up_got.astype(F32)
                down_part = down_part + down_got.astype(F32)
            up_got = lax.ppermute(up_part.astype(BF16), "z", up)
            down_got = lax.ppermute(down_part.astype(BF16), "z", down)
        (acts,) = call(act_body, [shaped((2 * count, wide))], [part[0], up_got, down_got])

        chunks = {0: acts}
        below = above = acts
        for step in range(1, half):
            below, above = lax.ppermute(below, "z", up), lax.ppermute(above, "z", down)
            chunks[step], chunks[nchip - step] = below, above
        top = lax.ppermute(below[:count], "z", up)
        bottom = lax.ppermute(above[count:], "z", down)
        own_acts, other_acts, parts = call(
            other_body,
            [shaped((nchip * count, wide))] * 2 + [shaped((nchip * count, 2 * d))],
            [chunks[k] for k in (0, 1, 2, 3, 5, 6, 7)] + [top, bottom, gate_up_w, down_weight],
            flops=2 * nchip * count * d * wide,
        )
        (sums,) = call(
            own_body,
            [shaped((nchip * count, 2 * d))],
            [own_acts, gate_up_w, down_weight, swap(parts)],
            flops=2 * nchip * count * d * wide,
        )
        back = between_chips(sums.reshape(nchip, count, 2 * d))
        gate_grad, up_grad, down_grad = call(
            grads_body,
            [shaped((d, hid))] * 3,
            [own.reshape(-1, 2 * d), other.reshape(-1, 2 * d), own_acts, other_acts],
            flops=4 * nchip * count * d * wide,
        )
        back = jnp.sum(back.astype(F32), axis=0).astype(BF16).reshape(WIN * nz, SLOTS, 2 * d)
        home = lax.all_to_all(back, ("w", "z"), 0, 0, tiled=True)
        home = home.reshape(WIN, nz, SLOTS, 2 * d).transpose(0, 2, 1, 3)
        in_rows = home[..., :d].reshape(WIN * SLOTS, nz * d)
        out_rows = home[..., d:].reshape(WIN * SLOTS, nz * d)

        layer_out = dot(weighted_b, out_rows, ((0,), (0,))).astype(BF16)
        tokens_grad = dot(plain_b, in_rows, ((0,), (0,))).astype(BF16)
        inner = jnp.sum(home_grad * out_rows.astype(F32), axis=1)
        by_token = plain * inner[:, None]
        combine_grad = jnp.zeros(combine.shape, F32)
        for expert in range(WIN):
            value = jnp.sum(by_token[expert * SLOTS : (expert + 1) * SLOTS], axis=0)
            combine_grad = combine_grad + jnp.where(matches[expert], value[:, None], 0.0)
        return layer_out, tokens_grad, combine_grad, gate_grad, up_grad, down_grad

    return shards


def solution(mesh):
    nexp, nz = mesh.devices.shape
    fine = Mesh(mesh.devices.reshape(WIN, 2, nexp // (4 * WIN), 2, nz), AXES)
    expert = AXES[:-1]
    row = P(expert + ("z",), None)
    weight = P("z", expert)
    return jax.shard_map(
        make_shards(nz, nexp // (2 * WIN)),
        mesh=fine,
        in_specs=(row, row, row, row, weight, weight, weight),
        out_specs=(row, row, row, weight, weight, weight),
        check_vma=False,
    )
```

```python
import jax
import jax.numpy as jnp
from jax import lax
from jax.experimental import pallas as pl
from jax.experimental.pallas import tpu as pltpu
from jax.sharding import Mesh
from jax.sharding import PartitionSpec as P

WIN = 2
SLOTS = 4
F32 = jnp.float32
BF16 = jnp.bfloat16
AXES = ("w", "yl", "x", "c", "z")
VMEM = pl.BlockSpec(memory_space=pltpu.VMEM)


def dot(left, right, contract):
    return lax.dot_general(left, right, (contract, ((), ())), preferred_element_type=F32)


def call(body, outs, args, scratch=(), flops=0):
    moved = sum(a.size * a.dtype.itemsize for a in args)
    moved += sum(s.size * s.dtype.itemsize for s in outs)
    return pl.pallas_call(
        body,
        out_shape=outs,
        in_specs=[VMEM] * len(args),
        out_specs=[VMEM] * len(outs),
        scratch_shapes=list(scratch),
        cost_estimate=pl.CostEstimate(flops=flops, bytes_accessed=moved, transcendentals=0),
        compiler_params=pltpu.CompilerParams(vmem_limit_bytes=48 * 1024 * 1024),
    )(*args)


def shaped(shape, dtype=BF16):
    return jax.ShapeDtypeStruct(shape, dtype)


def pick_rows(combine, expert_ids):
    combine_float = combine.astype(F32)
    slot_index = jnp.arange(SLOTS, dtype=jnp.int32)
    plain, weighted, all_matches = [], [], []
    for expert in range(WIN):
        matches = expert_ids == expert
        chosen = jnp.any(matches, axis=1)
        weight = jnp.sum(jnp.where(matches, combine_float, 0.0), axis=1)
        places = jnp.cumsum(chosen.astype(jnp.int32)) - 1
        picker = chosen[None, :] & (places[None, :] == slot_index[:, None])
        plain.append(picker.astype(F32))
        weighted.append(jnp.where(picker, weight[None, :], 0.0))
        all_matches.append(matches)
    return jnp.concatenate(plain), jnp.concatenate(weighted), all_matches


def first_body(own, other, gate_up_w, down_w, own_out, other_out):
    d = gate_up_w.shape[0]
    for rows, out in ((own, own_out), (other, other_out)):
        split = gate_up_w.shape[1]
        out[:, :split] = dot(rows[:, :d], gate_up_w[...], ((1,), (0,))).astype(BF16)
        out[:, split:] = dot(rows[:, d:], down_w[...], ((1,), (0,))).astype(BF16)


def pair_body(own_a, other_a, own_b, other_b, gate_up_w, down_w, *outs):
    split = gate_up_w.shape[1]
    d = gate_up_w.shape[0]
    half = own_a.shape[0]
    pairs = ((own_a, other_a), (own_b, other_b))[: len(outs)]
    rows = jnp.concatenate([ref[...] for pair in pairs for ref in pair])
    one = dot(rows[:, :d], gate_up_w[...], ((1,), (0,)))
    two = dot(rows[:, d:], down_w[...], ((1,), (0,)))
    for k, out in enumerate(outs):
        out[:, :split] = one[2 * k * half : 2 * (k + 1) * half]
        out[:, split:] = two[2 * k * half : 2 * (k + 1) * half]


def lead_body(up_part, down_part, up_got, down_got, up_out, down_out):
    count = up_got.shape[0]
    up_out[...] = (up_part[:count, :] + up_got[...].astype(F32)).astype(BF16)
    down_out[...] = (down_part[count:, :] + down_got[...].astype(F32)).astype(BF16)


def trail_body(up_part, down_part, up_got, down_got, up_out, down_out):
    count = up_got.shape[0]
    up_out[...] = (up_part[count:, :] + up_got[...].astype(F32)).astype(BF16)
    down_out[...] = (down_part[:count, :] + down_got[...].astype(F32)).astype(BF16)


def act_body(part, up_lead, down_lead, up_trail, down_trail, top, bottom):
    hid = part.shape[1] // 3
    count = part.shape[0] // 2
    for at_row, one, two, out in ((0, up_lead, down_trail, top), (count, up_trail, down_lead, bottom)):

        def total(at):
            cols = slice(at * hid, (at + 1) * hid)
            got = one[:, cols].astype(F32) + two[:, cols].astype(F32)
            return part[at_row : at_row + count, cols] + got

        gate_pre, up_pre, back = total(0), total(1), total(2)
        sigma = jax.nn.sigmoid(gate_pre)
        active = gate_pre * sigma
        out[:, 2 * hid :] = (active * up_pre).astype(BF16)
        out[:, hid : 2 * hid] = (back * active).astype(BF16)
        out[:, :hid] = (back * up_pre * sigma * (1.0 + gate_pre * (1.0 - sigma))).astype(BF16)


def other_body(*refs):
    tops, bottoms, (gate_up_w, down_w, own_acts, other_acts, parts) = refs[:8], refs[8:16], refs[16:]
    half = tops[0].shape[0]
    for k in range(8):
        own_acts[k * half : (k + 1) * half, :] = tops[k][...]
        other_acts[k * half : (k + 1) * half, :] = bottoms[k][...]
    d, split = gate_up_w.shape
    parts[:, :d] = dot(other_acts[:, :split], gate_up_w[...], ((1,), (1,))).astype(BF16)
    parts[:, d:] = dot(other_acts[:, split:], down_w[...], ((1,), (1,))).astype(BF16)


def own_body(own_acts, gate_up_w, down_w, got, parts):
    d, split = gate_up_w.shape
    one = dot(own_acts[:, :split], gate_up_w[...], ((1,), (1,)))
    parts[:, :d] = (one + got[:, :d].astype(F32)).astype(BF16)
    two = dot(own_acts[:, split:], down_w[...], ((1,), (1,)))
    parts[:, d:] = (two + got[:, d:].astype(F32)).astype(BF16)


def grads_body(own, other, own_acts, other_acts, gate_grad, up_grad, down_grad):
    d, hid = gate_grad.shape
    split = 2 * hid
    both = dot(own[:, :d], own_acts[:, :split], ((0,), (0,)))
    both = both + dot(other[:, :d], other_acts[:, :split], ((0,), (0,)))
    gate_grad[...] = both[:, :hid].astype(BF16)
    up_grad[...] = both[:, hid:].astype(BF16)
    last = dot(own[:, d:], own_acts[:, split:], ((0,), (0,)))
    last = last + dot(other[:, d:], other_acts[:, split:], ((0,), (0,)))
    down_grad[...] = last.astype(BF16)


def make_shards(nz, nchip):
    up = [(i, (i + 1) % nz) for i in range(nz)]
    down = [(i, (i - 1) % nz) for i in range(nz)]
    half = nz // 2
    groups = []
    for w in range(WIN):
        for c in range(2):
            for z in range(nz):
                chips = [(z - k) % nchip for k in range(nchip)]
                groups.append([((w * nchip + chip) * 2 + c) * nz + z for chip in chips])

    def between_chips(blocks):
        return lax.all_to_all(blocks, AXES, 0, 0, axis_index_groups=groups, tiled=True)

    def swap(block):
        return lax.ppermute(block, "c", [(0, 1), (1, 0)])

    def shards(tokens, output_grad, combine, expert_ids, gate_weight, up_weight, down_weight):
        d, hid = gate_weight.shape
        wide = 3 * hid
        plain, weighted, matches = pick_rows(combine, expert_ids)
        plain_b, weighted_b = plain.astype(BF16), weighted.astype(BF16)
        rows_x = dot(plain_b, tokens, ((1,), (0,))).astype(BF16)
        rows_g = dot(weighted_b, output_grad, ((1,), (0,))).astype(BF16)
        cut = lambda rows: rows.reshape(WIN, SLOTS, nz, d).transpose(0, 2, 1, 3)
        send = jnp.concatenate([cut(rows_x), cut(rows_g)], axis=3).reshape(WIN * nz, SLOTS, 2 * d)
        mine = lax.all_to_all(send, ("w", "z"), 0, 0, tiled=True)
        count = WIN * nz * SLOTS
        mine = mine.reshape(count, 2 * d)
        own = between_chips(jnp.broadcast_to(mine[None], (nchip, count, 2 * d)))
        other = swap(own)
        gate_up_w = jnp.concatenate([gate_weight, up_weight], axis=1)
        home_grad = dot(plain_b, output_grad, ((1,), (0,)))

        up_send, down_send = call(
            first_body,
            [shaped((count, wide))] * 2,
            [own[half], other[half], gate_up_w, down_weight],
            flops=4 * count * d * wide,
        )
        up_got = lax.ppermute(up_send, "z", up)
        down_got = lax.ppermute(down_send, "z", down)
        pairs = {}
        for away in range(half - 1, -1, -1):
            ups = (nchip - away) % nchip
            pairs[away] = call(
                pair_body,
                [shaped((2 * count, wide), F32)] * (2 if away else 1),
                [own[ups], other[ups], own[away], other[away], gate_up_w, down_weight],
                flops=8 * count * d * wide,
            )
        outs = [shaped((count, wide))] * 2
        up_part, down_part = pairs[half - 1]
        up_trail = lax.ppermute(up_part[count:].astype(BF16), "z", up)
        down_trail = lax.ppermute(down_part[:count].astype(BF16), "z", down)
        for away in range(half - 1, 0, -1):
            up_sum, down_sum = call(lead_body, outs, [*pairs[away], up_got, down_got])
            up_got = lax.ppermute(up_sum, "z", up)
            down_got = lax.ppermute(down_sum, "z", down)
            if away > 1:
                up_sum, down_sum = call(trail_body, outs, [*pairs[away - 1], up_trail, down_trail])
                up_trail = lax.ppermute(up_sum, "z", up)
                down_trail = lax.ppermute(down_sum, "z", down)
        top, bottom = call(act_body, outs, [pairs[0][0], up_got, down_got, up_trail, down_trail])

        tops, bottoms = {0: top}, {0: bottom}
        top_up = top_down = top
        bottom_up = bottom_down = bottom
        for step in range(1, half + 1):
            top_up = tops[step] = lax.ppermute(top_up, "z", up)
            bottom_down = bottoms[nchip - step] = lax.ppermute(bottom_down, "z", down)
            if step < half:
                bottom_up = bottoms[step] = lax.ppermute(bottom_up, "z", up)
                top_down = tops[nchip - step] = lax.ppermute(top_down, "z", down)
        own_acts, other_acts, parts = call(
            other_body,
            [shaped((nchip * count, wide))] * 2 + [shaped((nchip * count, 2 * d))],
            [each[k] for each in (tops, bottoms) for k in range(nchip)] + [gate_up_w, down_weight],
            flops=2 * nchip * count * d * wide,
        )
        (sums,) = call(
            own_body,
            [shaped((nchip * count, 2 * d))],
            [own_acts, gate_up_w, down_weight, swap(parts)],
            flops=2 * nchip * count * d * wide,
        )
        back = between_chips(sums.reshape(nchip, count, 2 * d))
        gate_grad, up_grad, down_grad = call(
            grads_body,
            [shaped((d, hid))] * 3,
            [own.reshape(-1, 2 * d), other.reshape(-1, 2 * d), own_acts, other_acts],
            flops=4 * nchip * count * d * wide,
        )
        back = jnp.sum(back.astype(F32), axis=0).astype(BF16).reshape(WIN * nz, SLOTS, 2 * d)
        home = lax.all_to_all(back, ("w", "z"), 0, 0, tiled=True)
        home = home.reshape(WIN, nz, SLOTS, 2 * d).transpose(0, 2, 1, 3)
        in_rows = home[..., :d].reshape(WIN * SLOTS, nz * d)
        out_rows = home[..., d:].reshape(WIN * SLOTS, nz * d)

        layer_out = dot(weighted_b, out_rows, ((0,), (0,))).astype(BF16)
        tokens_grad = dot(plain_b, in_rows, ((0,), (0,))).astype(BF16)
        inner = jnp.sum(home_grad * out_rows.astype(F32), axis=1)
        by_token = plain * inner[:, None]
        combine_grad = jnp.zeros(combine.shape, F32)
        for expert in range(WIN):
            value = jnp.sum(by_token[expert * SLOTS : (expert + 1) * SLOTS], axis=0)
            combine_grad = combine_grad + jnp.where(matches[expert], value[:, None], 0.0)
        return layer_out, tokens_grad, combine_grad, gate_grad, up_grad, down_grad

    return shards


def solution(mesh):
    nexp, nz = mesh.devices.shape
    fine = Mesh(mesh.devices.reshape(WIN, 2, nexp // (4 * WIN), 2, nz), AXES)
    expert = AXES[:-1]
    row = P(expert + ("z",), None)
    weight = P("z", expert)
    return jax.shard_map(
        make_shards(nz, nexp // (2 * WIN)),
        mesh=fine,
        in_specs=(row, row, row, row, weight, weight, weight),
        out_specs=(row, row, row, weight, weight, weight),
        check_vma=False,
    )
```
